512 devices in a mesh: inner: 32 (over z_lo, y, core), outer: 16 (over x, z_hi).
Axes of the slice: x: 4, y: 8, z: 8 (z_hi: 4, z_lo: 2; z = z_hi * 2 + z_lo), core: 2. Of those that a mesh axis runs over, the one named last changes fastest.
Arguments:
- gradients: bfloat16 [32, 16, 256, 8192], P('inner', 'outer'), may hold values from -6 to 6
- master_shard: float32 [256, 8192], P('outer', 'inner'), may hold values from -6 to 6
- first_moment: float32 [256, 8192], P('outer', 'inner'), may hold values from -48 to 48
- second_moment: float32 [256, 8192], P('outer', 'inner'), may hold values from 100 to 1000
Outputs:
- new_master: float32 [256, 8192], P('outer', 'inner')
- new_first: float32 [256, 8192], P('outer', 'inner')
- new_second: float32 [256, 8192], P('outer', 'inner')
- group_weights: bfloat16 [256, 8192], P(None, 'inner')
The draws below stay inside these ranges and needn't reach their ends.
All inputs are finite; a program needn't handle non-finite values.
Results may differ from the reference program's by a relative error of at most 0.0025.
Values may be sent and summed in bfloat16 or wider, within the bound.
A program may use at most 64 MiB of HBM per device.

```python
import math
import jax
import jax.numpy as jnp
from jax import lax

D = 8192
ROWS = 256
N_INNER = 32
N_OUTER = 16


def spiked(result, stream_key, source, target, shards_of, factor):
    owner, partner = [(jnp.arange(result.shape[position]) // (result.shape[position] // shards_of)).reshape([-1 if axis == position else 1 for axis in range(result.ndim)]) for position in (source, target)]
    chosen = jax.random.permutation(stream_key, shards_of)[partner]
    strong = (owner == chosen) | (owner == (partner + shards_of // 2) % shards_of)
    return jnp.where(strong, factor * result, result)


def steps_of(rng, dims, shards, least, high):
    level = 1.0
    for axis_at, parts in shards:
        heights = jax.random.uniform(jax.random.fold_in(jax.random.fold_in(rng, 6), axis_at), (parts,), jnp.float32, least / len(shards), high / len(shards))
        level = level * jnp.repeat(jnp.exp(heights), dims[axis_at] // parts).reshape((-1,) + (1,) * (len(dims) - 1 - axis_at))
    return level


def centred(stream_key, extent, spread, bound, cuts=(), dtype=jnp.bfloat16):
    drawn = spread * jax.random.normal(stream_key, extent, jnp.float32)
    if cuts:
        drawn = drawn * steps_of(stream_key, extent, cuts, -0.22, 0.18)
    return jnp.clip(drawn, -bound, bound).astype(dtype)


def noise_with(stream_key, extent, width, bound, shards, heavy, held_as=jnp.bfloat16):
    values = width * jax.random.normal(stream_key, extent, jnp.float32)
    if shards:
        values = values * steps_of(stream_key, extent, shards, -0.22, 0.18)
    return jnp.clip(spiked(values, jax.random.fold_in(stream_key, 3), *heavy), -bound, bound).astype(held_as)


def setup_inputs(seed: int = 0) -> dict:
    arg_keys = jax.random.split(jax.random.key(seed), 5)
    gradients = noise_with(arg_keys[0], (N_INNER, N_OUTER, ROWS, D), 1.0, 6.0, ((0, 32), (1, 16)), (1, 2, 16, 2.0))
    master_shard = centred(arg_keys[1], (ROWS, D), 1.0, 6.0, ((0, 16), (1, 32)), jnp.float32)
    first_moment = centred(arg_keys[2], (ROWS, D), 8.0, 48.0, ((0, 16), (1, 32)), jnp.float32)
    second_moment = jnp.clip(jnp.exp(math.log(1000.0) - 2.3025851 * jax.random.uniform(arg_keys[3], (ROWS, D), jnp.float32) ** steps_of(arg_keys[3], (ROWS, D), ((0, 16), (1, 32)), -0.2, 0.2)), 100.0, 1000.0)
    return dict(gradients=gradients, master_shard=master_shard, first_moment=first_moment, second_moment=second_moment)


beta_first = 0.9
beta_second = 0.95
learn_rate = 0.05
decay_rate = 0.1
adam_eps = 1e-05
bias_first = 1.0 - 0.9 ** 10
bias_second = 1.0 - 0.95 ** 10

def reference(gradients, master_shard, first_moment, second_moment):
    total = lax.optimization_barrier(jnp.sum(gradients.astype(jnp.float32), axis=(0, 1)))
    new_first = beta_first * first_moment + (1.0 - beta_first) * total
    new_second = beta_second * second_moment + (1.0 - beta_second) * total * total
    update = new_first / bias_first / (jnp.sqrt(new_second / bias_second) + adam_eps) + decay_rate * master_shard
    new_master = master_shard - learn_rate * update
    group_weights = new_master.astype(jnp.bfloat16)
    return (new_master, new_first, new_second, group_weights)
```

```python
import jax
import jax.numpy as jnp
from jax import lax
from jax.experimental import pallas as pl
from jax.experimental.pallas import tpu as pltpu
from jax.sharding import PartitionSpec as P

MESH = pl.DeviceIdType.MESH
F32 = jnp.float32
BF16 = jnp.bfloat16

beta_first = 0.9
beta_second = 0.95
learn_rate = 0.05
decay_rate = 0.1
adam_eps = 1e-05
bias_first = 1.0 - 0.9**10
bias_second = 1.0 - 0.95**10

NX, NY, NZ = 4, 8, 8


def device(x, y, z, core):
    return ((z % 2) * 16 + y * 2 + core, x * 4 + z // 2)


def adam(total, master, first, second):
    new_first = beta_first * first + (1.0 - beta_first) * total
    new_second = beta_second * second + (1.0 - beta_second) * total * total
    update = (
        new_first / bias_first / (jnp.sqrt(new_second / bias_second) + adam_eps)
        + decay_rate * master
    )
    return master - learn_rate * update, new_first, new_second


def kernel(
    grad, master_in, first_in, second_in,
    master_out, first_out, second_out, weights_out,
    own, other, sent_a, got_a, sent_y, got_y, sent_z, got_z,
    part_a, got_a2, sum_a, got_a3,
    part_y, part_z, got_h2, sum_h, got_h3,
    state, result, weights,
    load_sem, state_sem, store_sem,
    core_s, core_r, a_s, a_r, y_s, y_r, z_s, z_r,
    a2_s, a2_r, h2_s, h2_r, a3_s, a3_r, h3_s, h3_r, w_s, w_r,
):
    inner = lax.axis_index("inner")
    outer = lax.axis_index("outer")
    core = inner % 2
    y = (inner // 2) % NY
    x = outer // 4
    z_hi = outer % 4
    z_lo = inner // 16
    z = z_hi * 2 + z_lo
    odd = (y + z) % 2

    def at_x(d):
        return device((x + d) % NX, y, z, core)

    def at_y(d):
        return device(x, (y + d) % NY, z, core)

    def at_z(d):
        return device(x, y, (z + d) % NZ, core)

    def remote(src, dst, send, recv, target):
        return pltpu.make_async_remote_copy(
            src_ref=src, dst_ref=dst, send_sem=send, recv_sem=recv,
            device_id=target, device_id_type=MESH,
        )

    barrier = pltpu.get_barrier_semaphore()
    peers = (
        [device(x, y, z, 1 - core)]
        + [at_x(d) for d in range(1, NX)]
        + [at_y(d) for d in range(1, NY)]
        + [at_z(d) for d in range(1, NZ)]
    )
    for peer in peers:
        pl.semaphore_signal(barrier, inc=1, device_id=peer, device_id_type=MESH)

    def column(p, i, which):
        cy = (y + 1 + i) % NY
        start = (((cy + p) % 2) * 16 + cy * 2 + which) * 256
        return pl.ds(pl.multiple_of(start, 256), 256)

    def load(p, i):
        return pltpu.make_async_copy(
            grad.at[:, column(p, i, core)], own.at[p, i], load_sem.at[p, i]
        )

    def swap(p, i):
        return remote(
            grad.at[:, column(p, i, 1 - core)], other.at[p, i],
            core_s.at[p, i], core_r.at[p, i], device(x, y, z, 1 - core),
        )

    def each(count, step):
        def body(i, carry):
            step(i)
            return carry

        lax.fori_loop(0, count, body, 0)

    for p in range(2):
        each(NY, lambda i: load(p, i).start())
    states = [
        pltpu.make_async_copy(ref, state.at[n], state_sem.at[n])
        for n, ref in enumerate((master_in, first_in, second_in))
    ]
    for copy in states:
        copy.start()

    pl.semaphore_wait(barrier, len(peers))
    for p in range(2):
        each(NY, lambda i: swap(p, i).start())

    def send_a(p, k):
        return remote(
            sent_a.at[p, k], got_a.at[p, k - 1],
            a_s.at[p, k - 1], a_r.at[p, k - 1], at_x(k),
        )

    def send_y(p, d):
        return remote(
            sent_y.at[(y + d) % NY, p], got_y.at[d - 1, p],
            y_s.at[p, d - 1], y_r.at[p, d - 1], at_y(d),
        )

    def send_z(p, d):
        return remote(
            sent_z.at[(z + d) % NZ, p], got_z.at[d - 1, p],
            z_s.at[p, d - 1], z_r.at[p, d - 1], at_z(d),
        )

    for p in range(2):

        def chip_sum(i):
            load(p, i).wait()
            swap(p, i).wait_recv()
            cy = (y + 1 + i) % NY
            cz = (cy + p) % 2
            for k in range(NX):
                rows = pl.ds(pl.multiple_of(((x + k) % NX) * 64, 64), 64)
                value = (
                    own[p, i, rows, :].astype(F32) + other[p, i, rows, :].astype(F32)
                ).astype(BF16)
                sent_a[p, k, cy] = value[:, :128]
                if k % 2 == 1:
                    sent_y[cy, p, k // 2] = value[:, 128:]
                else:
                    for hi in range(4):
                        sent_z[hi * 2 + cz, p, cy // 2, k // 2] = value[
                            hi * 16 : hi * 16 + 16, 128:
                        ]

            @pl.when(i < NY - 1)
            def _():
                send_y(p, i + 1).start()

        each(NY, chip_sum)
        for k in range(1, NX):
            send_a(p, k).start()
        each(NZ - 1, lambda i: send_z(p, i + 1).start())

    def send_a2(p, d):
        if p == 0:
            src, target = part_a.at[p, (y + d) % NY], at_y(d)
        else:
            src, target = part_a.at[p, (z + d) % NZ], at_z(d)
        return remote(
            src, got_a2.at[p, d - 1], a2_s.at[p, d - 1], a2_r.at[p, d - 1], target
        )

    for p in range(2):
        for k in range(1, NX):
            send_a(p, k).wait_recv()

        def x_sum(cy):
            value = sent_a[p, 0, cy].astype(F32)
            for k in range(NX - 1):
                value += got_a[p, k, cy].astype(F32)
            value = value.astype(BF16)
            for hi in range(4):
                if p == 0:
                    part_a[p, cy, hi] = value[hi * 16 : hi * 16 + 16]
                else:
                    part_a[p, hi * 2 + (cy + 1) % 2, cy // 2] = value[hi * 16 : hi * 16 + 16]

        each(NY, x_sum)
        each(NY - 1, lambda i: send_a2(p, i + 1).start())

    def send_h2(way, d):
        if way == 0:
            src, target = part_y.at[(z + d) % NZ], at_z(d)
        else:
            src, target = part_z.at[(y + d) % NY], at_y(d)
        return remote(
            src, got_h2.at[way, d - 1], h2_s.at[way, d - 1], h2_r.at[way, d - 1], target
        )

    for p in range(2):
        each(NY - 1, lambda i: send_y(p, i + 1).wait_recv())
        for k in range(2):
            value = sent_y[y, p, k].astype(F32)
            for d in range(NY - 1):
                value += got_y[d, p, k].astype(F32)
            value = value.astype(BF16)
            for hi in range(4):
                part_y[hi * 2 + (y + p) % 2, k] = value[hi * 16 : hi * 16 + 16]
    each(NZ - 1, lambda i: send_h2(0, i + 1).start())

    for p in range(2):
        each(NZ - 1, lambda i: send_z(p, i + 1).wait_recv())

        def z_sum(ci):
            for k in range(2):
                value = sent_z[z, p, ci, k].astype(F32)
                for d in range(NZ - 1):
                    value += got_z[d, p, ci, k].astype(F32)
                part_z[2 * ci + (z + p) % 2, k] = value.astype(BF16)

        each(4, z_sum)
    each(NY - 1, lambda i: send_h2(1, i + 1).start())

    def send_a3(d):
        along_z = (odd + d + 1) % 2
        to_y = (y + (1 - along_z) * d) % NY
        to_z = (z + along_z * d) % NZ
        index = (along_z * to_z + (1 - along_z) * to_y) // 2
        return remote(
            sum_a.at[1 - along_z, index], got_a3.at[d - 1],
            a3_s.at[d - 1], a3_r.at[d - 1], device(x, to_y, to_z, core),
        )

    for p in range(2):
        each(NY - 1, lambda i: send_a2(p, i + 1).wait_recv())
        for n in range(4):
            value = part_a[p, y if p == 0 else z, n].astype(F32)
            for d in range(NY - 1):
                value += got_a2[p, d, n].astype(F32)
            sum_a[p, n] = value.astype(BF16)
    each(NY - 1, lambda i: send_a3(i + 1).start())

    def send_h3(k):
        return remote(
            sum_h.at[k], got_h3.at[k - 1], h3_s.at[k - 1], h3_r.at[k - 1], at_x(k)
        )

    for way in range(2):
        each(NZ - 1, lambda i: send_h2(way, i + 1).wait_recv())
        for k in range(2):
            value = (part_y[z, k] if way == 0 else part_z[y, k]).astype(F32)
            for d in range(NZ - 1):
                value += got_h2[way, d, k].astype(F32)
            sum_h[2 * k + 1 - way] = value.astype(BF16)
    for k in range(1, NX):
        send_h3(k).start()

    for copy in states:
        copy.wait()

    def finish(half, total):
        cols = slice(half * 128, half * 128 + 128)
        new_master, new_first, new_second = adam(
            total, state[0, :, cols], state[1, :, cols], state[2, :, cols]
        )
        result[0, :, cols] = new_master
        result[1, :, cols] = new_first
        result[2, :, cols] = new_second
        weights[:, cols] = new_master.astype(BF16)

    for k in range(1, NX):
        send_h3(k).wait_recv()
    total = sum_h[0].astype(F32)
    for k in range(NX - 1):
        total += got_h3[k].astype(F32)
    finish(1, total)

    each(NY - 1, lambda i: send_a3(i + 1).wait_recv())
    last = (z * (1 - odd) + y * odd) // 2
    total = sum_a[odd, last].astype(F32)
    for d in range(NY - 1):
        total += got_a3[d].astype(F32)
    finish(0, total)

    rows = pl.ds(pl.multiple_of(outer * 16, 16), 16)

    def spread(n):
        return remote(
            weights, weights_out.at[rows], w_s.at[n - 1], w_r.at[n - 1],
            (inner, ((x + n // 4) % 4) * 4 + (z_hi + n % 4) % 4),
        )

    def arrive(n):
        source = ((x - n // 4 + 4) % 4) * 4 + (z_hi - n % 4 + 4) % 4
        return remote(
            weights, weights_out.at[pl.ds(pl.multiple_of(source * 16, 16), 16)],
            w_s.at[n - 1], w_r.at[n - 1], (inner, source),
        )

    each(15, lambda i: spread(i + 1).start())
    stores = [
        pltpu.make_async_copy(result.at[n], ref, store_sem.at[n])
        for n, ref in enumerate((master_out, first_out, second_out))
    ] + [pltpu.make_async_copy(weights, weights_out.at[rows], store_sem.at[3])]
    for copy in stores:
        copy.start()

    for p in range(2):
        each(NY, lambda i: swap(p, i).wait_send())
        for k in range(1, NX):
            send_a(p, k).wait_send()
        each(NY - 1, lambda i: send_y(p, i + 1).wait_send())
        each(NY - 1, lambda i: send_z(p, i + 1).wait_send())
        each(NY - 1, lambda i: send_a2(p, i + 1).wait_send())
        each(NY - 1, lambda i: send_h2(p, i + 1).wait_send())
    each(NY - 1, lambda i: send_a3(i + 1).wait_send())
    for k in range(1, NX):
        send_h3(k).wait_send()
    for copy in stores:
        copy.wait()
    each(15, lambda i: spread(i + 1).wait_send())
    each(15, lambda i: arrive(i + 1).wait_recv())


def body(gradients, master_shard, first_moment, second_moment):
    grad = gradients.reshape(gradients.shape[2], gradients.shape[3])
    hbm = pl.BlockSpec(memory_space=pltpu.HBM)
    dma = pltpu.SemaphoreType.DMA
    shard = jax.ShapeDtypeStruct(master_shard.shape, F32)
    return pl.pallas_call(
        kernel,
        out_shape=(shard, shard, shard, jax.ShapeDtypeStruct((256, 256), BF16)),
        in_specs=[hbm] * 4,
        out_specs=(hbm,) * 4,
        scratch_shapes=[
            pltpu.VMEM((2, 8, 256, 256), BF16),
            pltpu.VMEM((2, 8, 256, 256), BF16),
            pltpu.VMEM((2, 4, 8, 64, 128), BF16),
            pltpu.VMEM((2, 3, 8, 64, 128), BF16),
            pltpu.VMEM((8, 2, 2, 64, 128), BF16),
            pltpu.VMEM((7, 2, 2, 64, 128), BF16),
            pltpu.VMEM((8, 2, 4, 2, 16, 128), BF16),
            pltpu.VMEM((7, 2, 4, 2, 16, 128), BF16),
            pltpu.VMEM((2, 8, 4, 16, 128), BF16),
            pltpu.VMEM((2, 7, 4, 16, 128), BF16),
            pltpu.VMEM((2, 4, 16, 128), BF16),
            pltpu.VMEM((7, 16, 128), BF16),
            pltpu.VMEM((8, 2, 16, 128), BF16),
            pltpu.VMEM((8, 2, 16, 128), BF16),
            pltpu.VMEM((2, 7, 2, 16, 128), BF16),
            pltpu.VMEM((4, 16, 128), BF16),
            pltpu.VMEM((3, 16, 128), BF16),
            pltpu.VMEM((3, 16, 256), F32),
            pltpu.VMEM((3, 16, 256), F32),
            pltpu.VMEM((16, 256), BF16),
            dma((2, 8)), dma((3,)), dma((4,)),
            dma((2, 8)), dma((2, 8)),
            dma((2, 3)), dma((2, 3)),
            dma((2, 7)), dma((2, 7)),
            dma((2, 7)), dma((2, 7)),
            dma((2, 7)), dma((2, 7)),
            dma((2, 7)), dma((2, 7)),
            dma((7,)), dma((7,)),
            dma((3,)), dma((3,)),
            dma((15,)), dma((15,)),
        ],
        compiler_params=pltpu.CompilerParams(
            collective_id=0, has_side_effects=True, vmem_limit_bytes=63 << 20
        ),
        name="reduce_adam_gather",
    )(grad, master_shard, first_moment, second_moment)


def solution(mesh):
    return jax.shard_map(
        body,
        mesh=mesh,
        in_specs=(
            P("inner", "outer", None, None),
            P("outer", "inner"),
            P("outer", "inner"),
            P("outer", "inner"),
        ),
        out_specs=(P("outer", "inner"), P("outer", "inner"), P("outer", "inner"), P(None, "inner")),
        check_vma=False,
    )
```

```python
import jax
import jax.numpy as jnp
from jax import lax
from jax.experimental import pallas as pl
from jax.experimental.pallas import tpu as pltpu
from jax.sharding import PartitionSpec as P

MESH = pl.DeviceIdType.MESH
F32 = jnp.float32
BF16 = jnp.bfloat16

beta_first = 0.9
beta_second = 0.95
learn_rate = 0.05
decay_rate = 0.1
adam_eps = 1e-05
bias_first = 1.0 - 0.9**10
bias_second = 1.0 - 0.95**10

NX, NY, NZ = 4, 8, 8


def device(x, y, z, core):
    return ((z % 2) * 16 + y * 2 + core, x * 4 + z // 2)


def adam(total, master, first, second):
    new_first = beta_first * first + (1.0 - beta_first) * total
    new_second = beta_second * second + (1.0 - beta_second) * total * total
    update = (
        new_first / bias_first / (jnp.sqrt(new_second / bias_second) + adam_eps)
        + decay_rate * master
    )
    return master - learn_rate * update, new_first, new_second


def each(count, step, first=0):
    def body(i, carry):
        step(i)
        return carry

    lax.fori_loop(first, count, body, 0)


def distance(i):
    return (((i // 2 + 1) * (1 - 2 * (i % 2)) + 8) % 8) * (1 - i // 7)


def hops(n):
    return min(n // 4, 4 - n // 4) + 2 * min(n % 4, 4 - n % 4)


def kernel(
    grad, master_in, first_in, second_in,
    state_out, weights_out,
    own, other, sent_a, got_a, sent_y, got_y, sent_z, got_z,
    part_a, got_a2, sum_a, got_a3, part_h, got_h2, sum_h, got_h3,
    state, result, weights,
    load_sem, state_sem, store_sem, far_sem,
    core_s, core_r, a_s, a_r, y_s, y_r, z_s, z_r,
    a2_s, a2_r, h2_s, h2_r, a3_s, a3_r, h3_s, h3_r, w_s, w_r,
):
    inner = lax.axis_index("inner")
    outer = lax.axis_index("outer")
    core = inner % 2
    y = (inner // 2) % NY
    x = outer // 4
    z_hi = outer % 4
    z = z_hi * 2 + inner // 16
    odd = (y + z) % 2

    def at_x(d):
        return device((x + d) % NX, y, z, core)

    def at_y(d):
        return device(x, (y + d) % NY, z, core)

    def at_z(d):
        return device(x, y, (z + d) % NZ, core)

    sibling = device(x, y, z, 1 - core)

    def remote(src, dst, send, recv, target):
        return pltpu.make_async_remote_copy(
            src_ref=src, dst_ref=dst, send_sem=send, recv_sem=recv,
            device_id=target, device_id_type=MESH,
        )

    barrier = pltpu.get_barrier_semaphore()
    near = (
        [at_x(d) for d in (2, 1, 3)]
        + [at_y(d) for d in (2, 6, 1, 7)]
        + [at_z(d) for d in (2, 6, 1, 7)]
        + [sibling]
    )
    for peer in near:
        pl.semaphore_signal(barrier, inc=1, device_id=peer, device_id_type=MESH)

    def column(p, i, which):
        cy = (y + distance(i)) % NY
        start = (((cy + p) % 2) * 16 + cy * 2 + which) * 256
        return pl.ds(pl.multiple_of(start, 256), 256)

    def load(p, i):
        return pltpu.make_async_copy(
            grad.at[:, column(p, i, core)], own.at[p, i], load_sem.at[p, i]
        )

    def swap(p, i):
        return remote(
            grad.at[:, column(p, i, 1 - core)], other.at[p, i],
            core_s.at[p, i], core_r.at[p, i], sibling,
        )

    for p in range(2):
        each(NY, lambda i: load(p, i).start())
    states = [
        pltpu.make_async_copy(ref, state.at[n], state_sem.at[n])
        for n, ref in enumerate((master_in, first_in, second_in))
    ]
    for copy in states:
        copy.start()

    pl.semaphore_wait(barrier, len(near))
    two_away = (at_y(2), at_y(6), at_z(2), at_z(6))
    for n, peer in enumerate(two_away):
        pl.semaphore_signal(far_sem.at[n], inc=1, device_id=peer, device_id_type=MESH)
    for p in range(2):
        each(NY, lambda i: swap(p, i).start())

    def send_a(p, part, k):
        blocks = pl.ds(part * 4, 4)
        return remote(
            sent_a.at[p, k, blocks], got_a.at[p, k - 1, blocks],
            a_s.at[p, part, k - 1], a_r.at[p, part, k - 1], at_x(k),
        )

    def send_y(p, d):
        return remote(
            sent_y.at[(y + d) % NY, p], got_y.at[d - 1, p],
            y_s.at[p, d - 1], y_r.at[p, d - 1], at_y(d),
        )

    def send_z(p, d):
        return remote(
            sent_z.at[(z + d) % NZ, p], got_z.at[d - 1, p],
            z_s.at[p, d - 1], z_r.at[p, d - 1], at_z(d),
        )

    def chip_sum(p, i):
        load(p, i).wait()
        swap(p, i).wait_recv()
        cy = (y + distance(i)) % NY
        cz = (cy + p) % 2
        for k in range(NX):
            rows = pl.ds(pl.multiple_of(((x + k) % NX) * 64, 64), 64)
            value = own[p, i, rows, :] + other[p, i, rows, :]
            sent_a[p, k, i] = value[:, :128].reshape(4, 16, 128)
            if k % 2 == 1:
                sent_y[cy, p, k // 2] = value[:, 128:].reshape(4, 16, 128)
            else:
                for hi in range(4):
                    sent_z[hi * 2 + cz, p, cy // 2, k // 2] = value[
                        hi * 16 : hi * 16 + 16, 128:
                    ]

    for p in range(2):

        def step(i):
            chip_sum(p, i)
            send_y(p, distance(i)).start()

        each(4, step)
        for k in range(1, NX):
            send_a(p, 0, k).start()
        if p == 0:
            for n in range(4):
                pl.semaphore_wait(far_sem.at[n], 1)
        each(7, step, first=4)
        chip_sum(p, 7)
        for k in range(1, NX):
            send_a(p, 1, k).start()
        each(7, lambda i: send_z(p, distance(i)).start())

    def send_a2(p, d):
        if p == 0:
            src, target = part_a.at[p, (y + d) % NY], at_y(d)
        else:
            src, target = part_a.at[p, (z + d) % NZ], at_z(d)
        return remote(
            src, got_a2.at[p, d - 1], a2_s.at[p, d - 1], a2_r.at[p, d - 1], target
        )

    def send_h2(way, d):
        if way == 0:
            src, target = part_h.at[way, (z + d) % NZ], at_z(d)
        else:
            src, target = part_h.at[way, (y + d) % NY], at_y(d)
        return remote(
            src, got_h2.at[way, d - 1], h2_s.at[way, d - 1], h2_r.at[way, d - 1], target
        )

    def start_h2(way, p):
        mine, crossing = (z, y) if way == 0 else (y, z)

        def step(n):
            d = (2 * n + (crossing + p) % 2 - mine + 8) % 8

            @pl.when(d != 0)
            def _():
                send_h2(way, d).start()

        each(4, step)

    def x_sum(p, i):
        value = sent_a[p, 0, i].astype(F32)
        for k in range(NX - 1):
            value += got_a[p, k, i].astype(F32)
        value = value.astype(BF16)
        cy = (y + distance(i)) % NY
        if p == 0:
            part_a[p, cy] = value
        else:
            for hi in range(4):
                part_a[p, hi * 2 + (cy + 1) % 2, cy // 2] = value[hi]

    def first_sums(p):
        for part in range(2):
            for k in range(1, NX):
                send_a(p, part, k).wait_recv()

            def step(i):
                x_sum(p, i)
                if p == 0:
                    send_a2(p, distance(i)).start()

            each(4 + 3 * part, step, first=4 * part)
            if part == 1:
                x_sum(p, 7)
        if p == 1:
            each(7, lambda i: send_a2(p, distance(6 - i)).start())

        each(NY - 1, lambda i: send_y(p, i + 1).wait_recv())
        for k in range(2):
            value = sent_y[y, p, k].astype(F32)
            for d in range(NY - 1):
                value += got_y[d, p, k].astype(F32)
            value = value.astype(BF16)
            for hi in range(4):
                part_h[0, hi * 2 + (y + p) % 2, k] = value[hi]
        start_h2(0, p)

        each(NZ - 1, lambda i: send_z(p, i + 1).wait_recv())

        def z_sum(ci):
            value = sent_z[z, p, ci].astype(F32)
            for d in range(NZ - 1):
                value += got_z[d, p, ci].astype(F32)
            part_h[1, 2 * ci + (z + p) % 2] = value.astype(BF16)

        each(4, z_sum)
        start_h2(1, p)

    def last_a(p, d):
        to_y = y if p == 0 else (y + d) % NY
        to_z = (z + d) % NZ if p == 0 else z
        index = (to_z if p == 0 else to_y) // 2
        return remote(
            sum_a.at[p, index], got_a3.at[d - 1],
            a3_s.at[d - 1], a3_r.at[d - 1], device(x, to_y, to_z, core),
        )

    def second_sum_a(p):
        each(NY - 1, lambda i: send_a2(p, i + 1).wait_recv())
        value = part_a[p, y if p == 0 else z].astype(F32)
        for d in range(NY - 1):
            value += got_a2[p, d].astype(F32)
        sum_a[p] = value.astype(BF16)

        def step(n):
            d = 2 * n + (odd + p) % 2

            @pl.when(d != 0)
            def _():
                last_a(p, d).start()

        each(4, step)

    def send_h3(k):
        return remote(
            sum_h.at[k], got_h3.at[k - 1], h3_s.at[k - 1], h3_r.at[k - 1], at_x(k)
        )

    first_sums(0)
    first_sums(1)
    second_sum_a(0)
    for way in range(2):
        each(NZ - 1, lambda i: send_h2(way, i + 1).wait_recv())
        value = part_h[way, z if way == 0 else y].astype(F32)
        for d in range(NZ - 1):
            value += got_h2[way, d].astype(F32)
        value = value.astype(BF16)
        for k in range(2):
            sum_h[2 * k + 1 - way] = value[k]
    for k in range(1, NX):
        send_h3(k).start()
    second_sum_a(1)

    for copy in states:
        copy.wait()

    def finish(half, total):
        cols = slice(half * 128, half * 128 + 128)
        new_master, new_first, new_second = adam(
            total, state[0, :, cols], state[1, :, cols], state[2, :, cols]
        )
        result[0, :, cols] = new_master
        result[1, :, cols] = new_first
        result[2, :, cols] = new_second
        weights[:, cols] = new_master.astype(BF16)

    for k in range(1, NX):
        send_h3(k).wait_recv()
    total = sum_h[0].astype(F32)
    for k in range(NX - 1):
        total += got_h3[k].astype(F32)
    finish(1, total)

    each(NY - 1, lambda i: last_a(0, i + 1).wait_recv())
    total = sum_a[odd, (z * (1 - odd) + y * odd) // 2].astype(F32)
    for d in range(NY - 1):
        total += got_a3[d].astype(F32)
    finish(0, total)

    rows = pl.ds(pl.multiple_of(outer * 16, 16), 16)

    def spread(n):
        return remote(
            weights, weights_out.at[rows], w_s.at[n - 1], w_r.at[n - 1],
            (inner, ((x + n // 4) % 4) * 4 + (z_hi + n % 4) % 4),
        )

    def arrive(n):
        source = ((x - n // 4 + 4) % 4) * 4 + (z_hi - n % 4 + 4) % 4
        return remote(
            weights, weights_out.at[pl.ds(pl.multiple_of(source * 16, 16), 16)],
            w_s.at[n - 1], w_r.at[n - 1], (inner, source),
        )

    for n in sorted(range(1, 16), key=lambda n: -hops(n)):
        spread(n).start()
    stores = [
        pltpu.make_async_copy(result, state_out, store_sem.at[0]),
        pltpu.make_async_copy(weights, weights_out.at[rows], store_sem.at[1]),
    ]
    for copy in stores:
        copy.start()

    for p in range(2):
        each(NY, lambda i: swap(p, i).wait_send())
        for k in range(1, NX):
            for part in range(2):
                send_a(p, part, k).wait_send()
        each(NY - 1, lambda i: send_y(p, i + 1).wait_send())
        each(NY - 1, lambda i: send_z(p, i + 1).wait_send())
        each(NY - 1, lambda i: send_a2(p, i + 1).wait_send())
        each(NY - 1, lambda i: send_h2(p, i + 1).wait_send())
    each(NY - 1, lambda i: last_a(0, i + 1).wait_send())
    for k in range(1, NX):
        send_h3(k).wait_send()
    for copy in stores:
        copy.wait()
    each(15, lambda i: spread(i + 1).wait_send())
    each(15, lambda i: arrive(i + 1).wait_recv())


def hand_out(state, weights, master_out, first_out, second_out, weights_out, held, block, sem):
    fetch = [
        pltpu.make_async_copy(state, held, sem.at[0]),
        pltpu.make_async_copy(weights, block, sem.at[1]),
    ]
    copies = [
        pltpu.make_async_copy(held.at[n], ref, sem.at[2 + n])
        for n, ref in enumerate((master_out, first_out, second_out))
    ] + [pltpu.make_async_copy(block, weights_out, sem.at[5])]
    for copy in fetch:
        copy.start()
    fetch[1].wait()
    copies[3].start()
    fetch[0].wait()
    for copy in copies[:3]:
        copy.start()
    for copy in copies:
        copy.wait()


def body(gradients, master_shard, first_moment, second_moment):
    grad = gradients.reshape(gradients.shape[2], gradients.shape[3])
    hbm = pl.BlockSpec(memory_space=pltpu.HBM)
    dma = pltpu.SemaphoreType.DMA
    shard = jax.ShapeDtypeStruct(master_shard.shape, F32)
    group = jax.ShapeDtypeStruct((256, 256), BF16)
    state, weights = pl.pallas_call(
        kernel,
        out_shape=(jax.ShapeDtypeStruct((3,) + master_shard.shape, F32), group),
        in_specs=[hbm] * 4,
        out_specs=(hbm,) * 2,
        scratch_shapes=[
            pltpu.VMEM((2, 8, 256, 256), BF16),
            pltpu.VMEM((2, 8, 256, 256), BF16),
            pltpu.VMEM((2, 4, 8, 4, 16, 128), BF16),
            pltpu.VMEM((2, 3, 8, 4, 16, 128), BF16),
            pltpu.VMEM((8, 2, 2, 4, 16, 128), BF16),
            pltpu.VMEM((7, 2, 2, 4, 16, 128), BF16),
            pltpu.VMEM((8, 2, 4, 2, 16, 128), BF16),
            pltpu.VMEM((7, 2, 4, 2, 16, 128), BF16),
            pltpu.VMEM((2, 8, 4, 16, 128), BF16),
            pltpu.VMEM((2, 7, 4, 16, 128), BF16),
            pltpu.VMEM((2, 4, 16, 128), BF16),
            pltpu.VMEM((7, 16, 128), BF16),
            pltpu.VMEM((2, 8, 2, 16, 128), BF16),
            pltpu.VMEM((2, 7, 2, 16, 128), BF16),
            pltpu.VMEM((4, 16, 128), BF16),
            pltpu.VMEM((3, 16, 128), BF16),
            pltpu.VMEM((3, 16, 256), F32),
            pltpu.VMEM((3, 16, 256), F32),
            pltpu.VMEM((16, 256), BF16),
            dma((2, 8)), dma((3,)), dma((2,)), pltpu.SemaphoreType.REGULAR((4,)),
            dma((2, 8)), dma((2, 8)),
            dma((2, 2, 3)), dma((2, 2, 3)),
            dma((2, 7)), dma((2, 7)),
            dma((2, 7)), dma((2, 7)),
            dma((2, 7)), dma((2, 7)),
            dma((2, 7)), dma((2, 7)),
            dma((7,)), dma((7,)),
            dma((3,)), dma((3,)),
            dma((15,)), dma((15,)),
        ],
        compiler_params=pltpu.CompilerParams(
            collective_id=0, has_side_effects=True, vmem_limit_bytes=60 << 20
        ),
        name="reduce_adam_gather",
    )(grad, master_shard, first_moment, second_moment)
    return pl.pallas_call(
        hand_out,
        out_shape=(shard, shard, shard, group),
        in_specs=[hbm] * 2,
        out_specs=(hbm,) * 4,
        scratch_shapes=[
            pltpu.VMEM((3,) + master_shard.shape, F32), pltpu.VMEM((256, 256), BF16), dma((6,)),
        ],
        compiler_params=pltpu.CompilerParams(vmem_limit_bytes=60 << 20),
        name="hand_out",
    )(state, weights)


def solution(mesh):
    return jax.shard_map(
        body,
        mesh=mesh,
        in_specs=(
            P("inner", "outer", None, None),
            P("outer", "inner"),
            P("outer", "inner"),
            P("outer", "inner"),
        ),
        out_specs=(P("outer", "inner"), P("outer", "inner"), P("outer", "inner"), P(None, "inner")),
        check_vma=False,
    )
```

```python
import jax
import jax.numpy as jnp
from jax import lax
from jax.experimental import pallas as pl
from jax.experimental.pallas import tpu as pltpu
from jax.sharding import PartitionSpec as P

MESH = pl.DeviceIdType.MESH
F32 = jnp.float32
BF16 = jnp.bfloat16

beta_first = 0.9
beta_second = 0.95
learn_rate = 0.05
decay_rate = 0.1
adam_eps = 1e-05
bias_first = 1.0 - 0.9**10
bias_second = 1.0 - 0.95**10

NX, NY, NZ = 4, 8, 8


def device(x, y, z, core):
    return ((z % 2) * 16 + y * 2 + core, x * 4 + z // 2)


def adam(total, master, first, second):
    new_first = beta_first * first + (1.0 - beta_first) * total
    new_second = beta_second * second + (1.0 - beta_second) * total * total
    update = (
        new_first / bias_first / (jnp.sqrt(new_second / bias_second) + adam_eps)
        + decay_rate * master
    )
    return master - learn_rate * update, new_first, new_second


def each(count, step, first=0):
    def body(i, carry):
        step(i)
        return carry

    lax.fori_loop(first, count, body, 0)


def distance(i):
    return (((i // 2 + 1) * (1 - 2 * (i % 2)) + 8) % 8) * (1 - i // 7)


def hops(n):
    return min(n // 4, 4 - n // 4) + 2 * min(n % 4, 4 - n % 4)


def kernel(
    grad, master_in, first_in, second_in,
    state_out, weights_out,
    own, other, sent_a, got_a, sent_y, got_y, sent_z, got_z,
    part_a, got_a2, sum_a, got_a3, part_h, got_h2, sum_h, got_h3,
    state, result, weights,
    load_sem, state_sem, store_sem, far_sem,
    core_s, core_r, a_s, a_r, y_s, y_r, z_s, z_r,
    a2_s, a2_r, h2_s, h2_r, a3_s, a3_r, h3_s, h3_r, w_s, w_r,
):
    inner = lax.axis_index("inner")
    outer = lax.axis_index("outer")
    core = inner % 2
    y = (inner // 2) % NY
    x = outer // 4
    z_hi = outer % 4
    z = z_hi * 2 + inner // 16
    odd = (y + z) % 2

    def at_x(d):
        return device((x + d) % NX, y, z, core)

    def at_y(d):
        return device(x, (y + d) % NY, z, core)

    def at_z(d):
        return device(x, y, (z + d) % NZ, core)

    sibling = device(x, y, z, 1 - core)

    def remote(src, dst, send, recv, target):
        return pltpu.make_async_remote_copy(
            src_ref=src, dst_ref=dst, send_sem=send, recv_sem=recv,
            device_id=target, device_id_type=MESH,
        )

    barrier = pltpu.get_barrier_semaphore()
    near = (
        [at_x(d) for d in (2, 1, 3)]
        + [at_y(d) for d in (2, 6, 1, 7)]
        + [at_z(d) for d in (2, 6, 1, 7)]
        + [sibling]
    )
    for peer in near:
        pl.semaphore_signal(barrier, inc=1, device_id=peer, device_id_type=MESH)

    def column(p, i, which):
        cy = (y + distance(i)) % NY
        start = (((cy + p) % 2) * 16 + cy * 2 + which) * 256
        return pl.ds(pl.multiple_of(start, 256), 256)

    def load(p, i):
        return pltpu.make_async_copy(
            grad.at[:, column(p, i, core)], own.at[p, i], load_sem.at[p, i]
        )

    def swap(p, i):
        return remote(
            grad.at[:, column(p, i, 1 - core)], other.at[p, i],
            core_s.at[p, i], core_r.at[p, i], sibling,
        )

    for p in range(2):
        each(NY, lambda i: load(p, i).start())
    states = [
        pltpu.make_async_copy(ref, state.at[n], state_sem.at[n])
        for n, ref in enumerate((master_in, first_in, second_in))
    ]
    for copy in states:
        copy.start()

    pl.semaphore_wait(barrier, len(near))
    two_away = (at_y(2), at_y(6), at_z(2), at_z(6))
    for n, peer in enumerate(two_away):
        pl.semaphore_signal(far_sem.at[n], inc=1, device_id=peer, device_id_type=MESH)
    for p in range(2):
        each(NY, lambda i: swap(p, i).start())

    def send_a(p, part, k):
        blocks = pl.ds(part * 4, 4)
        return remote(
            sent_a.at[p, k, blocks], got_a.at[p, k - 1, blocks],
            a_s.at[p, part, k - 1], a_r.at[p, part, k - 1], at_x(k),
        )

    def send_y(p, d):
        return remote(
            sent_y.at[(y + d) % NY, p], got_y.at[d - 1, p],
            y_s.at[p, d - 1], y_r.at[p, d - 1], at_y(d),
        )

    def send_z(p, d):
        return remote(
            sent_z.at[(z + d) % NZ, p], got_z.at[d - 1, p],
            z_s.at[p, d - 1], z_r.at[p, d - 1], at_z(d),
        )

    def chip_sum(p, i):
        load(p, i).wait()
        swap(p, i).wait_recv()
        cy = (y + distance(i)) % NY
        cz = (cy + p) % 2
        for k in range(NX):
            rows = pl.ds(pl.multiple_of(((x + k) % NX) * 64, 64), 64)
            value = own[p, i, rows, :] + other[p, i, rows, :]
            sent_a[p, k, i] = value[:, :128].reshape(4, 16, 128)
            if k % 2 == 1:
                sent_y[cy, p, k // 2] = value[:, 128:].reshape(4, 16, 128)
            else:
                for hi in range(4):
                    sent_z[hi * 2 + cz, p, cy // 2, 1 - k // 2] = value[
                        hi * 16 : hi * 16 + 16, 128:
                    ]

    for p in range(2):

        def step(i):
            chip_sum(p, i)
            send_y(p, distance(i)).start()

        each(4, step)
        for k in range(1, NX):
            send_a(p, 0, k).start()
        if p == 0:
            for n in range(4):
                pl.semaphore_wait(far_sem.at[n], 1)
        each(7, step, first=4)
        chip_sum(p, 7)
        for k in range(1, NX):
            send_a(p, 1, k).start()
        each(7, lambda i: send_z(p, distance(i)).start())

    def send_a2(p, d):
        if p == 0:
            src, target = part_a.at[p, (y + d) % NY], at_y(d)
        else:
            src, target = part_a.at[p, (z + d) % NZ], at_z(d)
        return remote(
            src, got_a2.at[p, d - 1], a2_s.at[p, d - 1], a2_r.at[p, d - 1], target
        )

    def send_h2(p, k):
        return remote(
            part_h.at[1 - k % 2, k // 2 if k % 2 else 0, p], got_h2.at[k - 1, p],
            h2_s.at[p, k - 1], h2_r.at[p, k - 1], at_x(k),
        )

    def x_sum(p, i):
        value = sent_a[p, 0, i].astype(F32)
        for k in range(NX - 1):
            value += got_a[p, k, i].astype(F32)
        value = value.astype(BF16)
        cy = (y + distance(i)) % NY
        if p == 0:
            part_a[p, cy] = value
        else:
            for hi in range(4):
                part_a[p, hi * 2 + (cy + 1) % 2, cy // 2] = value[hi]

    def first_sums(p):
        for part in range(2):
            for k in range(1, NX):
                send_a(p, part, k).wait_recv()

            def step(i):
                x_sum(p, i)
                if p == 0:
                    send_a2(p, distance(i)).start()

            each(4 + 3 * part, step, first=4 * part)
            if part == 1:
                x_sum(p, 7)
        if p == 1:
            each(7, lambda i: send_a2(p, distance(6 - i)).start())

        each(NY - 1, lambda i: send_y(p, i + 1).wait_recv())
        for k in range(2):
            value = sent_y[y, p, k].astype(F32)
            for d in range(NY - 1):
                value += got_y[d, p, k].astype(F32)
            value = value.astype(BF16)
            part_h[0, k, p] = value
            send_h2(p, 2 * k + 1).start()

        each(NZ - 1, lambda i: send_z(p, i + 1).wait_recv())

        def z_sum(ci):
            value = sent_z[z, p, ci].astype(F32)
            for d in range(NZ - 1):
                value += got_z[d, p, ci].astype(F32)
            value = value.astype(BF16)
            for k in range(2):
                part_h[1, k, p, ci] = value[k]

        each(4, z_sum)
        send_h2(p, 2).start()

    def last_a(p, d):
        to_y = y if p == 0 else (y + d) % NY
        to_z = (z + d) % NZ if p == 0 else z
        index = (to_z if p == 0 else to_y) // 2
        return remote(
            sum_a.at[p, index], got_a3.at[d - 1],
            a3_s.at[d - 1], a3_r.at[d - 1], device(x, to_y, to_z, core),
        )

    def second_sum_a(p):
        each(NY - 1, lambda i: send_a2(p, i + 1).wait_recv())
        value = part_a[p, y if p == 0 else z].astype(F32)
        for d in range(NY - 1):
            value += got_a2[p, d].astype(F32)
        sum_a[p] = value.astype(BF16)

        def step(n):
            d = 2 * n + (odd + p) % 2

            @pl.when(d != 0)
            def _():
                last_a(p, d).start()

        each(4, step)

    def last_h(way, d):
        index = (z + d) % NZ if way == 0 else (y + d) % NY
        return remote(
            sum_h.at[way, index], got_h3.at[way, d - 1],
            h3_s.at[way, d - 1], h3_r.at[way, d - 1], at_z(d) if way == 0 else at_y(d),
        )

    def second_sum_h(p):
        for k in range(1, NX):
            send_h2(p, k).wait_recv()
        for way in range(2):
            first = (got_h2[0, p] if way == 0 else part_h[1, 1, p]).astype(F32)
            value = (first + got_h2[2 - way, p].astype(F32)).astype(BF16)
            for n in range(4):
                sum_h[way, 2 * n + ((y if way == 0 else z) + p) % 2] = value[n]

            def step(n):
                d = 2 * n + (odd + p) % 2

                @pl.when(d != 0)
                def _():
                    last_h(way, d).start()

            each(4, step)

    first_sums(0)
    first_sums(1)
    second_sum_a(0)
    second_sum_h(0)
    second_sum_h(1)
    second_sum_a(1)

    for copy in states:
        copy.wait()

    def finish(half, total):
        cols = slice(half * 128, half * 128 + 128)
        new_master, new_first, new_second = adam(
            total, state[0, :, cols], state[1, :, cols], state[2, :, cols]
        )
        result[0, :, cols] = new_master
        result[1, :, cols] = new_first
        result[2, :, cols] = new_second
        weights[:, cols] = new_master.astype(BF16)

    for way in range(2):
        each(NY - 1, lambda i: last_h(way, i + 1).wait_recv())
    total = sum_h[0, z].astype(F32) + sum_h[1, y].astype(F32)
    for way in range(2):
        for d in range(NY - 1):
            total += got_h3[way, d].astype(F32)
    finish(1, total)

    each(NY - 1, lambda i: last_a(0, i + 1).wait_recv())
    total = sum_a[odd, (z * (1 - odd) + y * odd) // 2].astype(F32)
    for d in range(NY - 1):
        total += got_a3[d].astype(F32)
    finish(0, total)

    rows = pl.ds(pl.multiple_of(outer * 16, 16), 16)

    def spread(n):
        return remote(
            weights, weights_out.at[rows], w_s.at[n - 1], w_r.at[n - 1],
            (inner, ((x + n // 4) % 4) * 4 + (z_hi + n % 4) % 4),
        )

    def arrive(n):
        source = ((x - n // 4 + 4) % 4) * 4 + (z_hi - n % 4 + 4) % 4
        return remote(
            weights, weights_out.at[pl.ds(pl.multiple_of(source * 16, 16), 16)],
            w_s.at[n - 1], w_r.at[n - 1], (inner, source),
        )

    for n in sorted(range(1, 16), key=lambda n: -hops(n)):
        spread(n).start()
    stores = [
        pltpu.make_async_copy(result, state_out, store_sem.at[0]),
        pltpu.make_async_copy(weights, weights_out.at[rows], store_sem.at[1]),
    ]
    for copy in stores:
        copy.start()

    for p in range(2):
        each(NY, lambda i: swap(p, i).wait_send())
        for k in range(1, NX):
            for part in range(2):
                send_a(p, part, k).wait_send()
        each(NY - 1, lambda i: send_y(p, i + 1).wait_send())
        each(NY - 1, lambda i: send_z(p, i + 1).wait_send())
        each(NY - 1, lambda i: send_a2(p, i + 1).wait_send())
        for k in range(1, NX):
            send_h2(p, k).wait_send()
        each(NY - 1, lambda i: last_h(p, i + 1).wait_send())
    each(NY - 1, lambda i: last_a(0, i + 1).wait_send())
    for copy in stores:
        copy.wait()
    each(15, lambda i: spread(i + 1).wait_send())
    each(15, lambda i: arrive(i + 1).wait_recv())


def hand_out(state, weights, master_out, first_out, second_out, weights_out, held, block, sem):
    fetch = [
        pltpu.make_async_copy(state, held, sem.at[0]),
        pltpu.make_async_copy(weights, block, sem.at[1]),
    ]
    copies = [
        pltpu.make_async_copy(held.at[n], ref, sem.at[2 + n])
        for n, ref in enumerate((master_out, first_out, second_out))
    ] + [pltpu.make_async_copy(block, weights_out, sem.at[5])]
    for copy in fetch:
        copy.start()
    fetch[1].wait()
    copies[3].start()
    fetch[0].wait()
    for copy in copies[:3]:
        copy.start()
    for copy in copies:
        copy.wait()


def body(gradients, master_shard, first_moment, second_moment):
    grad = gradients.reshape(gradients.shape[2], gradients.shape[3])
    hbm = pl.BlockSpec(memory_space=pltpu.HBM)
    dma = pltpu.SemaphoreType.DMA
    shard = jax.ShapeDtypeStruct(master_shard.shape, F32)
    group = jax.ShapeDtypeStruct((256, 256), BF16)
    state, weights = pl.pallas_call(
        kernel,
        out_shape=(jax.ShapeDtypeStruct((3,) + master_shard.shape, F32), group),
        in_specs=[hbm] * 4,
        out_specs=(hbm,) * 2,
        scratch_shapes=[
            pltpu.VMEM((2, 8, 256, 256), BF16),
            pltpu.VMEM((2, 8, 256, 256), BF16),
            pltpu.VMEM((2, 4, 8, 4, 16, 128), BF16),
            pltpu.VMEM((2, 3, 8, 4, 16, 128), BF16),
            pltpu.VMEM((8, 2, 2, 4, 16, 128), BF16),
            pltpu.VMEM((7, 2, 2, 4, 16, 128), BF16),
            pltpu.VMEM((8, 2, 4, 2, 16, 128), BF16),
            pltpu.VMEM((7, 2, 4, 2, 16, 128), BF16),
            pltpu.VMEM((2, 8, 4, 16, 128), BF16),
            pltpu.VMEM((2, 7, 4, 16, 128), BF16),
            pltpu.VMEM((2, 4, 16, 128), BF16),
            pltpu.VMEM((7, 16, 128), BF16),
            pltpu.VMEM((2, 2, 2, 4, 16, 128), BF16),
            pltpu.VMEM((3, 2, 4, 16, 128), BF16),
            pltpu.VMEM((2, 8, 16, 128), BF16),
            pltpu.VMEM((2, 7, 16, 128), BF16),
            pltpu.VMEM((3, 16, 256), F32),
            pltpu.VMEM((3, 16, 256), F32),
            pltpu.VMEM((16, 256), BF16),
            dma((2, 8)), dma((3,)), dma((2,)), pltpu.SemaphoreType.REGULAR((4,)),
            dma((2, 8)), dma((2, 8)),
            dma((2, 2, 3)), dma((2, 2, 3)),
            dma((2, 7)), dma((2, 7)),
            dma((2, 7)), dma((2, 7)),
            dma((2, 7)), dma((2, 7)),
            dma((2, 3)), dma((2, 3)),
            dma((7,)), dma((7,)),
            dma((2, 7)), dma((2, 7)),
            dma((15,)), dma((15,)),
        ],
        compiler_params=pltpu.CompilerParams(
            collective_id=0, has_side_effects=True, vmem_limit_bytes=60 << 20
        ),
        name="reduce_adam_gather",
    )(grad, master_shard, first_moment, second_moment)
    return pl.pallas_call(
        hand_out,
        out_shape=(shard, shard, shard, group),
        in_specs=[hbm] * 2,
        out_specs=(hbm,) * 4,
        scratch_shapes=[
            pltpu.VMEM((3,) + master_shard.shape, F32), pltpu.VMEM((256, 256), BF16), dma((6,)),
        ],
        compiler_params=pltpu.CompilerParams(vmem_limit_bytes=60 << 20),
        name="hand_out",
    )(state, weights)


def solution(mesh):
    return jax.shard_map(
        body,
        mesh=mesh,
        in_specs=(
            P("inner", "outer", None, None),
            P("outer", "inner"),
            P("outer", "inner"),
            P("outer", "inner"),
        ),
        out_specs=(P("outer", "inner"), P("outer", "inner"), P("outer", "inner"), P(None, "inner")),
        check_vma=False,
    )
```

```python
import jax
import jax.numpy as jnp
from jax import lax
from jax.experimental import pallas as pl
from jax.experimental.pallas import tpu as pltpu
from jax.sharding import PartitionSpec as P

MESH = pl.DeviceIdType.MESH
F32 = jnp.float32
BF16 = jnp.bfloat16

beta_first = 0.9
beta_second = 0.95
learn_rate = 0.05
decay_rate = 0.1
adam_eps = 1e-05
bias_first = 1.0 - 0.9**10
bias_second = 1.0 - 0.95**10

NX, NY, NZ = 4, 8, 8


def mod(value, n):
    return value % n if isinstance(value, int) else lax.rem(value, jnp.int32(n))


def div(value, n):
    return value // n if isinstance(value, int) else lax.div(value, jnp.int32(n))


def adam(total, master, first, second):
    new_first = beta_first * first + (1.0 - beta_first) * total
    new_second = beta_second * second + (1.0 - beta_second) * total * total
    update = (
        new_first / bias_first / (jnp.sqrt(new_second / bias_second) + adam_eps)
        + decay_rate * master
    )
    return master - learn_rate * update, new_first, new_second


def each(count, step, first=0):
    def body(i, carry):
        step(i)
        return carry

    lax.fori_loop(first, count, body, 0)


def distance(i):
    return mod((div(i, 2) + 1) * (1 - 2 * mod(i, 2)) + 8, 8) * (1 - div(i, 7))


FAR_FIRST = (4, 3, 5, 2, 6, 1, 7)


def hops(n):
    return min(n // 4, 4 - n // 4) + 2 * min(n % 4, 4 - n % 4)


def kernel(
    grad, master_in, first_in, second_in,
    state_out, weights_out,
    own, other, sent_a, got_a, sent_y, got_y, sent_z, got_z,
    part_a, got_a2, sum_a, got_a3, part_h, got_h2, sum_h, got_h3,
    state, result, weights,
    load_sem, state_sem, store_sem, far_sem,
    core_s, core_r, a_s, a_r, y_s, y_r, z_s, z_r,
    a2_s, a2_r, h2_s, h2_r, a3_s, a3_r, h3_s, h3_r, w_s, w_r,
):
    inner = lax.axis_index("inner")
    outer = lax.axis_index("outer")
    core = mod(inner, 2)
    y = mod(div(inner, 2), NY)
    z_lo = div(inner, 16)
    x = div(outer, 4)
    z_hi = mod(outer, 4)
    z = z_hi * 2 + z_lo
    odd = mod(y + z, 2)

    def at_x(d):
        return (inner, mod(x + d, NX) * 4 + z_hi)

    def at_y(d):
        return (z_lo * 16 + mod(y + d, NY) * 2 + core, outer)

    def at_z(d):
        other_z = mod(z + d, NZ)
        return (mod(other_z, 2) * 16 + y * 2 + core, x * 4 + div(other_z, 2))

    sibling = (inner + 1 - 2 * core, outer)

    def arrived(ref, sem):
        pltpu.make_async_copy(ref, ref, sem).wait()

    def remote(src, dst, send, recv, target):
        return pltpu.make_async_remote_copy(
            src_ref=src, dst_ref=dst, send_sem=send, recv_sem=recv,
            device_id=target, device_id_type=MESH,
        )

    barrier = pltpu.get_barrier_semaphore()
    near = (
        [at_x(d) for d in (2, 1, 3)]
        + [at_y(d) for d in (2, 6, 1, 7)]
        + [at_z(d) for d in (2, 6, 1, 7)]
        + [sibling]
    )
    for peer in near:
        pl.semaphore_signal(barrier, inc=1, device_id=peer, device_id_type=MESH)

    def column(p, i, which):
        cy = mod(y + distance(i), NY)
        start = (mod(cy + p, 2) * 16 + cy * 2 + which) * 256
        return pl.ds(pl.multiple_of(start, 256), 256)

    def load(p, i):
        return pltpu.make_async_copy(
            grad.at[:, column(p, i, core)], own.at[p, i], load_sem.at[p, i]
        )

    def swap(p, i):
        return remote(
            grad.at[:, column(p, i, 1 - core)], other.at[p, i],
            core_s.at[0], core_r.at[p, i], sibling,
        )

    for p in range(2):
        each(NY, lambda i: load(p, i).start())
    states = [
        pltpu.make_async_copy(ref, state.at[n], state_sem.at[n])
        for n, ref in enumerate((master_in, first_in, second_in))
    ]
    for copy in states:
        copy.start()

    pl.semaphore_wait(barrier, len(near))
    two_away = (at_y(2), at_y(6), at_z(2), at_z(6))
    for n, peer in enumerate(two_away):
        pl.semaphore_signal(far_sem.at[n], inc=1, device_id=peer, device_id_type=MESH)
    for p in range(2):
        each(NY, lambda i: swap(p, i).start())

    def send_a(p, part, k):
        blocks = pl.ds(part * 4, 4)
        return remote(
            sent_a.at[p, k, blocks], got_a.at[p, k - 1, blocks],
            a_s.at[0], a_r.at[p, part], at_x(k),
        )

    def send_y(p, d):
        return remote(
            sent_y.at[mod(y + d, NY), p], got_y.at[d - 1, p],
            y_s.at[0], y_r.at[p], at_y(d),
        )

    def send_z(p, d):
        return remote(
            sent_z.at[mod(z + d, NZ), p], got_z.at[d - 1, p],
            z_s.at[0], z_r.at[p], at_z(d),
        )

    def chip_sum(p, i):
        load(p, i).wait()
        swap(p, i).wait_recv()
        cy = mod(y + distance(i), NY)
        cz = mod(cy + p, 2)
        for k in range(NX):
            rows = pl.ds(pl.multiple_of(mod(x + k, NX) * 64, 64), 64)
            value = own[p, i, rows, :] + other[p, i, rows, :]
            sent_a[p, k, i] = value[:, :128].reshape(4, 16, 128)
            if k % 2 == 1:
                sent_y[cy, p, k // 2] = value[:, 128:].reshape(4, 16, 128)
            else:
                for hi in range(4):
                    sent_z[hi * 2 + cz, p, div(cy, 2), 1 - k // 2] = value[
                        hi * 16 : hi * 16 + 16, 128:
                    ]

    for p in range(2):

        def step(i):
            chip_sum(p, i)
            send_y(p, distance(i)).start()

        each(4, step)
        for k in range(1, NX):
            send_a(p, 0, k).start()
        if p == 0:
            for n in range(4):
                pl.semaphore_wait(far_sem.at[n], 1)
        each(7, step, first=4)
        chip_sum(p, 7)
        for k in range(1, NX):
            send_a(p, 1, k).start()
        for d in FAR_FIRST:
            send_z(p, d).start()

    def send_a2(p, d):
        if p == 0:
            src, target = part_a.at[p, mod(y + d, NY)], at_y(d)
        else:
            src, target = part_a.at[p, mod(z + d, NZ)], at_z(d)
        return remote(
            src, got_a2.at[p, d - 1], a2_s.at[0], a2_r.at[p], target
        )

    def send_h2(p, k):
        return remote(
            part_h.at[1 - k % 2, k // 2 if k % 2 else 0, p], got_h2.at[k - 1, p],
            h2_s.at[0], h2_r.at[p], at_x(k),
        )

    def x_sum(p, i):
        value = sent_a[p, 0, i].astype(F32)
        for k in range(NX - 1):
            value += got_a[p, k, i].astype(F32)
        value = value.astype(BF16)
        cy = mod(y + distance(i), NY)
        if p == 0:
            part_a[p, cy] = value
        else:
            for hi in range(4):
                part_a[p, hi * 2 + mod(cy + 1, 2), div(cy, 2)] = value[hi]

    def first_sums(p):
        for part in range(2):
            arrived(got_a.at[p, :, pl.ds(4 * part, 4)], a_r.at[p, part])
            each(4 + 4 * part, lambda i: x_sum(p, i), first=4 * part)
        for d in FAR_FIRST:
            send_a2(p, d).start()

        arrived(got_y.at[:, p], y_r.at[p])
        for k in range(2):
            value = sent_y[y, p, k].astype(F32)
            for d in range(NY - 1):
                value += got_y[d, p, k].astype(F32)
            value = value.astype(BF16)
            part_h[0, k, p] = value
            send_h2(p, 2 * k + 1).start()

        arrived(got_z.at[:, p], z_r.at[p])

        def z_sum(ci):
            value = sent_z[z, p, ci].astype(F32)
            for d in range(NZ - 1):
                value += got_z[d, p, ci].astype(F32)
            value = value.astype(BF16)
            for k in range(2):
                part_h[1, k, p, ci] = value[k]

        each(4, z_sum)
        send_h2(p, 2).start()

    def last_a(p, d):
        to_y = y if p == 0 else mod(y + d, NY)
        to_z = mod(z + d, NZ) if p == 0 else z
        index = div(to_z if p == 0 else to_y, 2)
        return remote(
            sum_a.at[p, index], got_a3.at[d - 1],
            a3_s.at[0], a3_r.at[0], at_z(d) if p == 0 else at_y(d),
        )

    def to_owners(p, act):
        shift = mod(odd + p, 2)
        for n in (2, 1, 3):
            act(2 * n + shift)

        @pl.when(shift != 0)
        def _():
            act(shift)

    def second_sum_a(p):
        arrived(got_a2.at[p], a2_r.at[p])
        value = part_a[p, y if p == 0 else z].astype(F32)
        for d in range(NY - 1):
            value += got_a2[p, d].astype(F32)
        sum_a[p] = value.astype(BF16)

        to_owners(p, lambda d: last_a(p, d).start())

    def last_h(way, d):
        index = mod(z + d, NZ) if way == 0 else mod(y + d, NY)
        return remote(
            sum_h.at[way, index], got_h3.at[way, d - 1],
            h3_s.at[0], h3_r.at[way], at_z(d) if way == 0 else at_y(d),
        )

    def second_sum_h(p):
        arrived(got_h2.at[:, p], h2_r.at[p])
        for way in range(2):
            first = (got_h2[0, p] if way == 0 else part_h[1, 1, p]).astype(F32)
            value = (first + got_h2[2 - way, p].astype(F32)).astype(BF16)
            for n in range(4):
                sum_h[way, 2 * n + mod((y if way == 0 else z) + p, 2)] = value[n]

            to_owners(p, lambda d: last_h(way, d).start())

    first_sums(0)
    first_sums(1)
    second_sum_a(0)
    second_sum_h(0)
    second_sum_h(1)
    second_sum_a(1)

    for copy in states:
        copy.wait()

    def finish(half, total):
        cols = slice(half * 128, half * 128 + 128)
        new_master, new_first, new_second = adam(
            total, state[0, :, cols], state[1, :, cols], state[2, :, cols]
        )
        result[0, :, cols] = new_master
        result[1, :, cols] = new_first
        result[2, :, cols] = new_second
        weights[:, cols] = new_master.astype(BF16)

    for way in range(2):
        arrived(got_h3.at[way], h3_r.at[way])
    total = sum_h[0, z].astype(F32) + sum_h[1, y].astype(F32)
    for way in range(2):
        for d in range(NY - 1):
            total += got_h3[way, d].astype(F32)
    finish(1, total)

    arrived(got_a3, a3_r.at[0])
    total = sum_a[odd, div(z * (1 - odd) + y * odd, 2)].astype(F32)
    for d in range(NY - 1):
        total += got_a3[d].astype(F32)
    finish(0, total)

    rows = pl.ds(pl.multiple_of(outer * 16, 16), 16)

    def spread(n):
        return remote(
            weights, weights_out.at[rows], w_s.at[0], w_r.at[0],
            (inner, mod(x + n // 4, 4) * 4 + mod(z_hi + n % 4, 4)),
        )

    for n in sorted(range(1, 16), key=lambda n: -hops(n)):
        spread(n).start()
    stores = [
        pltpu.make_async_copy(result, state_out, store_sem.at[0]),
        pltpu.make_async_copy(weights, weights_out.at[rows], store_sem.at[1]),
    ]
    for copy in stores:
        copy.start()

    for ref, sem in (
        (other, core_s), (sent_a.at[:, pl.ds(1, 3)], a_s), (got_y, y_s), (got_z, z_s),
        (got_a2, a2_s), (got_h2, h2_s), (got_a3, a3_s), (got_h3, h3_s),
        (weights_out.at[pl.ds(0, 240)], w_s),
    ):
        arrived(ref, sem.at[0])
    for copy in stores:
        copy.wait()
    arrived(weights_out.at[pl.ds(0, 240)], w_r.at[0])


def hand_out(state, weights, master_out, first_out, second_out, weights_out, sem):
    copies = [
        pltpu.make_async_copy(state.at[n], ref, sem.at[n])
        for n, ref in enumerate((master_out, first_out, second_out))
    ] + [pltpu.make_async_copy(weights, weights_out, sem.at[3])]
    for copy in copies:
        copy.start()
    for copy in copies:
        copy.wait()


def body(gradients, master_shard, first_moment, second_moment):
    grad = gradients.reshape(gradients.shape[2], gradients.shape[3])
    hbm = pl.BlockSpec(memory_space=pltpu.HBM)
    dma = pltpu.SemaphoreType.DMA
    shard = jax.ShapeDtypeStruct(master_shard.shape, F32)
    group = jax.ShapeDtypeStruct((256, 256), BF16)
    state, weights = pl.pallas_call(
        kernel,
        out_shape=(jax.ShapeDtypeStruct((3,) + master_shard.shape, F32), group),
        in_specs=[hbm] * 4,
        out_specs=(hbm,) * 2,
        scratch_shapes=[
            pltpu.VMEM((2, 8, 256, 256), BF16),
            pltpu.VMEM((2, 8, 256, 256), BF16),
            pltpu.VMEM((2, 4, 8, 4, 16, 128), BF16),
            pltpu.VMEM((2, 3, 8, 4, 16, 128), BF16),
            pltpu.VMEM((8, 2, 2, 4, 16, 128), BF16),
            pltpu.VMEM((7, 2, 2, 4, 16, 128), BF16),
            pltpu.VMEM((8, 2, 4, 2, 16, 128), BF16),
            pltpu.VMEM((7, 2, 4, 2, 16, 128), BF16),
            pltpu.VMEM((2, 8, 4, 16, 128), BF16),
            pltpu.VMEM((2, 7, 4, 16, 128), BF16),
            pltpu.VMEM((2, 4, 16, 128), BF16),
            pltpu.VMEM((7, 16, 128), BF16),
            pltpu.VMEM((2, 2, 2, 4, 16, 128), BF16),
            pltpu.VMEM((3, 2, 4, 16, 128), BF16),
            pltpu.VMEM((2, 8, 16, 128), BF16),
            pltpu.VMEM((2, 7, 16, 128), BF16),
            pltpu.VMEM((3, 16, 256), F32),
            pltpu.VMEM((3, 16, 256), F32),
            pltpu.VMEM((16, 256), BF16),
            dma((2, 8)), dma((3,)), dma((2,)), pltpu.SemaphoreType.REGULAR((4,)),
            dma((1,)), dma((2, 8)),
            dma((1,)), dma((2, 2)),
            dma((1,)), dma((2,)),
            dma((1,)), dma((2,)),
            dma((1,)), dma((2,)),
            dma((1,)), dma((2,)),
            dma((1,)), dma((1,)),
            dma((1,)), dma((2,)),
            dma((1,)), dma((1,)),
        ],
        compiler_params=pltpu.CompilerParams(
            collective_id=0, has_side_effects=True, vmem_limit_bytes=52 << 20
        ),
        name="reduce_adam_gather",
    )(*[pltpu.with_memory_space_constraint(v, pltpu.HBM) for v in (grad, master_shard, first_moment, second_moment)])
    return pl.pallas_call(
        hand_out,
        out_shape=(shard, shard, shard, group),
        in_specs=[hbm] * 2,
        out_specs=(hbm,) * 4,
        scratch_shapes=[dma((4,))],
        compiler_params=pltpu.CompilerParams(vmem_limit_bytes=52 << 20),
        name="hand_out",
    )(state, weights)


def solution(mesh):
    return jax.shard_map(
        body,
        mesh=mesh,
        in_specs=(
            P("inner", "outer", None, None),
            P("outer", "inner"),
            P("outer", "inner"),
            P("outer", "inner"),
        ),
        out_specs=(P("outer", "inner"), P("outer", "inner"), P("outer", "inner"), P(None, "inner")),
        check_vma=False,
    )
```

```python
import jax
import jax.numpy as jnp
from jax import lax
from jax.experimental import pallas as pl
from jax.experimental.pallas import tpu as pltpu
from jax.sharding import PartitionSpec as P

MESH = pl.DeviceIdType.MESH
F32 = jnp.float32
BF16 = jnp.bfloat16

beta_first = 0.9
beta_second = 0.95
learn_rate = 0.05
decay_rate = 0.1
adam_eps = 1e-05
bias_first = 1.0 - 0.9**10
bias_second = 1.0 - 0.95**10

NX, NY, NZ = 4, 8, 8


def mod(value, n):
    return value % n if isinstance(value, int) else lax.rem(value, jnp.int32(n))


def div(value, n):
    return value // n if isinstance(value, int) else lax.div(value, jnp.int32(n))


def adam(total, master, first, second):
    new_first = beta_first * first + (1.0 - beta_first) * total
    new_second = beta_second * second + (1.0 - beta_second) * total * total
    update = (
        new_first / bias_first / (jnp.sqrt(new_second / bias_second) + adam_eps)
        + decay_rate * master
    )
    return master - learn_rate * update, new_first, new_second


def each(count, step, first=0):
    def body(i, carry):
        step(i)
        return carry

    lax.fori_loop(first, count, body, 0)


def distance(i):
    return mod((div(i, 2) + 1) * (1 - 2 * mod(i, 2)) + 8, 8) * (1 - div(i, 7))


FAR_FIRST = (4, 3, 5, 2, 6, 1, 7)


def hops(n):
    return min(n // 4, 4 - n // 4) + 2 * min(n % 4, 4 - n % 4)


def kernel(
    grad, master_in, first_in, second_in,
    state_out, weights_out,
    own, other, sent_a, got_a, sent_y, got_y, sent_z, got_z,
    part_a, got_a2, sum_a, got_a3, part_h, got_h2, sum_h, got_h3,
    state, result, weights,
    load_sem, state_sem, store_sem, far_sem, x_r,
    core_s, core_r, a_s, a_r, y_s, y_r, z_s, z_r,
    a2_s, a2_r, h2_s, h2_r, a3_s, a3_r, h3_s, h3_r, w_s, w_r,
):
    inner = lax.axis_index("inner")
    outer = lax.axis_index("outer")
    core = mod(inner, 2)
    y = mod(div(inner, 2), NY)
    z_lo = div(inner, 16)
    x = div(outer, 4)
    z_hi = mod(outer, 4)
    z = z_hi * 2 + z_lo
    odd = mod(y + z, 2)

    def at_x(d):
        return (inner, mod(x + d, NX) * 4 + z_hi)

    def at_y(d):
        return (z_lo * 16 + mod(y + d, NY) * 2 + core, outer)

    def at_z(d):
        other_z = mod(z + d, NZ)
        return (mod(other_z, 2) * 16 + y * 2 + core, x * 4 + div(other_z, 2))

    sibling = (inner + 1 - 2 * core, outer)

    def arrived(ref, sem):
        pltpu.make_async_copy(ref, ref, sem).wait()

    def remote(src, dst, send, recv, target):
        return pltpu.make_async_remote_copy(
            src_ref=src, dst_ref=dst, send_sem=send, recv_sem=recv,
            device_id=target, device_id_type=MESH,
        )

    barrier = pltpu.get_barrier_semaphore()
    near = (
        [at_x(d) for d in (2, 1, 3)]
        + [at_y(d) for d in (2, 6, 1, 7)]
        + [at_z(d) for d in (2, 6, 1, 7)]
        + [sibling]
    )
    for peer in near:
        pl.semaphore_signal(barrier, inc=1, device_id=peer, device_id_type=MESH)

    def column(p, i, which):
        cy = mod(y + distance(i), NY)
        start = (mod(cy + p, 2) * 16 + cy * 2 + which) * 256
        return pl.ds(pl.multiple_of(start, 256), 256)

    def load(p, i):
        return pltpu.make_async_copy(
            grad.at[:, column(p, i, core)], own.at[p, i], load_sem.at[p, i]
        )

    def swap(p, i):
        return remote(
            grad.at[:, column(p, i, 1 - core)], other.at[p, i],
            core_s.at[0], core_r.at[p, i], sibling,
        )

    for p in range(2):
        each(NY, lambda i: load(p, i).start())
    states = [
        pltpu.make_async_copy(ref, state.at[n], state_sem.at[n])
        for n, ref in enumerate((master_in, first_in, second_in))
    ]
    for copy in states:
        copy.start()

    pl.semaphore_wait(barrier, len(near))
    two_away = (at_y(2), at_y(6), at_z(2), at_z(6))
    for n, peer in enumerate(two_away):
        pl.semaphore_signal(far_sem.at[n], inc=1, device_id=peer, device_id_type=MESH)
    for p in range(2):
        each(NY, lambda i: swap(p, i).start())

    def pass_x(p, way, n):
        k = 2 if n == 0 else 1 + 2 * way
        blocks = pl.ds(4 * (way if n != 1 else 1 - way), 4)
        return remote(
            sent_a.at[p, k, blocks], got_a.at[p, min(n, 1), way, max(n - 1, 0)],
            a_s.at[0], a_r.at[p, min(n, 1)] if n else x_r.at[p, way], at_x(1 + 2 * way),
        )

    def start_x(p, part):
        pass_x(p, part, 0).start()
        pass_x(p, 1 - part, 1).start()

    def forward_x(p):
        for way in range(2):
            pass_x(p, way, 0).wait_recv()
            for i in range(4):
                sent_a[p, 1 + 2 * way, 4 * way + i] += got_a[p, 0, way, 0, i]
            pass_x(p, way, 2).start()

    def send_y(p, d):
        return remote(
            sent_y.at[mod(y + d, NY), p], got_y.at[d - 1, p],
            y_s.at[0], y_r.at[p], at_y(d),
        )

    def send_z(p, d):
        return remote(
            sent_z.at[mod(z + d, NZ), p], got_z.at[d - 1, p],
            z_s.at[0], z_r.at[p], at_z(d),
        )

    def chip_sum(p, i):
        load(p, i).wait()
        swap(p, i).wait_recv()
        cy = mod(y + distance(i), NY)
        cz = mod(cy + p, 2)
        for k in range(NX):
            rows = pl.ds(pl.multiple_of(mod(x + k, NX) * 64, 64), 64)
            value = own[p, i, rows, :] + other[p, i, rows, :]
            sent_a[p, k, i] = value[:, :128].reshape(4, 16, 128)
            if k % 2 == 1:
                sent_y[cy, p, k // 2] = value[:, 128:].reshape(4, 16, 128)
            else:
                for hi in range(4):
                    sent_z[hi * 2 + cz, p, div(cy, 2), 1 - k // 2] = value[
                        hi * 16 : hi * 16 + 16, 128:
                    ]

    for p in range(2):

        def step(i):
            chip_sum(p, i)
            send_y(p, distance(i)).start()

        each(4, step)
        start_x(p, 0)
        if p == 0:
            for n in range(4):
                pl.semaphore_wait(far_sem.at[n], 1)
        each(7, step, first=4)
        chip_sum(p, 7)
        start_x(p, 1)
        if p == 1:
            forward_x(0)
        for d in FAR_FIRST:
            send_z(p, d).start()

    forward_x(1)

    def send_a2(p, d):
        if p == 0:
            src, target = part_a.at[p, mod(y + d, NY)], at_y(d)
        else:
            src, target = part_a.at[p, mod(z + d, NZ)], at_z(d)
        return remote(
            src, got_a2.at[p, d - 1], a2_s.at[0], a2_r.at[p], target
        )

    def send_h2(p, k):
        return remote(
            part_h.at[1 - k % 2, k // 2 if k % 2 else 0, p], got_h2.at[k - 1, p],
            h2_s.at[0], h2_r.at[p], at_x(k),
        )

    def x_sum(p, i, part):
        value = sent_a[p, 0, i].astype(F32)
        for way in range(2):
            value += got_a[p, 1, way, 1 if way == part else 0, i - 4 * part].astype(F32)
        value = value.astype(BF16)
        cy = mod(y + distance(i), NY)
        if p == 0:
            part_a[p, cy] = value
        else:
            for hi in range(4):
                part_a[p, hi * 2 + mod(cy + 1, 2), div(cy, 2)] = value[hi]

    def first_sums(p):
        arrived(got_a.at[p, 1], a_r.at[p, 1])
        for part in range(2):
            each(4 + 4 * part, lambda i: x_sum(p, i, part), first=4 * part)
        for d in FAR_FIRST:
            send_a2(p, d).start()

        arrived(got_y.at[:, p], y_r.at[p])
        for k in range(2):
            value = sent_y[y, p, k].astype(F32)
            for d in range(NY - 1):
                value += got_y[d, p, k].astype(F32)
            value = value.astype(BF16)
            part_h[0, k, p] = value
            send_h2(p, 2 * k + 1).start()

        arrived(got_z.at[:, p], z_r.at[p])

        def z_sum(ci):
            value = sent_z[z, p, ci].astype(F32)
            for d in range(NZ - 1):
                value += got_z[d, p, ci].astype(F32)
            value = value.astype(BF16)
            for k in range(2):
                part_h[1, k, p, ci] = value[k]

        each(4, z_sum)
        send_h2(p, 2).start()

    def last_a(p, d):
        to_y = y if p == 0 else mod(y + d, NY)
        to_z = mod(z + d, NZ) if p == 0 else z
        index = div(to_z if p == 0 else to_y, 2)
        return remote(
            sum_a.at[p, index], got_a3.at[d - 1],
            a3_s.at[0], a3_r.at[0], at_z(d) if p == 0 else at_y(d),
        )

    def to_owners(p, act):
        shift = mod(odd + p, 2)
        for n in (2, 1, 3):
            act(2 * n + shift)

        @pl.when(shift != 0)
        def _():
            act(shift)

    def second_sum_a(p):
        arrived(got_a2.at[p], a2_r.at[p])
        value = part_a[p, y if p == 0 else z].astype(F32)
        for d in range(NY - 1):
            value += got_a2[p, d].astype(F32)
        sum_a[p] = value.astype(BF16)

        to_owners(p, lambda d: last_a(p, d).start())

    def last_h(way, d):
        index = mod(z + d, NZ) if way == 0 else mod(y + d, NY)
        return remote(
            sum_h.at[way, index], got_h3.at[way, d - 1],
            h3_s.at[0], h3_r.at[way], at_z(d) if way == 0 else at_y(d),
        )

    def second_sum_h(p):
        arrived(got_h2.at[:, p], h2_r.at[p])
        for way in range(2):
            first = (got_h2[0, p] if way == 0 else part_h[1, 1, p]).astype(F32)
            value = (first + got_h2[2 - way, p].astype(F32)).astype(BF16)
            for n in range(4):
                sum_h[way, 2 * n + mod((y if way == 0 else z) + p, 2)] = value[n]

            to_owners(p, lambda d: last_h(way, d).start())

    first_sums(0)
    first_sums(1)
    second_sum_a(0)
    second_sum_h(0)
    second_sum_h(1)
    second_sum_a(1)

    for copy in states:
        copy.wait()

    def finish(half, total):
        cols = slice(half * 128, half * 128 + 128)
        new_master, new_first, new_second = adam(
            total, state[0, :, cols], state[1, :, cols], state[2, :, cols]
        )
        result[0, :, cols] = new_master
        result[1, :, cols] = new_first
        result[2, :, cols] = new_second
        weights[:, cols] = new_master.astype(BF16)

    for way in range(2):
        arrived(got_h3.at[way], h3_r.at[way])
    total = sum_h[0, z].astype(F32) + sum_h[1, y].astype(F32)
    for way in range(2):
        for d in range(NY - 1):
            total += got_h3[way, d].astype(F32)
    finish(1, total)

    arrived(got_a3, a3_r.at[0])
    total = sum_a[odd, div(z * (1 - odd) + y * odd, 2)].astype(F32)
    for d in range(NY - 1):
        total += got_a3[d].astype(F32)
    finish(0, total)

    rows = pl.ds(pl.multiple_of(outer * 16, 16), 16)

    def spread(n):
        return remote(
            weights, weights_out.at[rows], w_s.at[0], w_r.at[0],
            (inner, mod(x + n // 4, 4) * 4 + mod(z_hi + n % 4, 4)),
        )

    for n in sorted(range(1, 16), key=lambda n: -hops(n)):
        spread(n).start()
    stores = [
        pltpu.make_async_copy(result, state_out, store_sem.at[0]),
        pltpu.make_async_copy(weights, weights_out.at[rows], store_sem.at[1]),
    ]
    for copy in stores:
        copy.start()

    for ref, sem in (
        (other, core_s), (sent_a.at[:, pl.ds(1, 3)], a_s), (got_y, y_s), (got_z, z_s),
        (got_a2, a2_s), (got_h2, h2_s), (got_a3, a3_s), (got_h3, h3_s),
        (weights_out.at[pl.ds(0, 240)], w_s),
    ):
        arrived(ref, sem.at[0])
    for copy in stores:
        copy.wait()
    arrived(weights_out.at[pl.ds(0, 240)], w_r.at[0])


def hand_out(state, weights, master_out, first_out, second_out, weights_out, sem):
    copies = [
        pltpu.make_async_copy(state.at[n], ref, sem.at[n])
        for n, ref in enumerate((master_out, first_out, second_out))
    ] + [pltpu.make_async_copy(weights, weights_out, sem.at[3])]
    for copy in copies:
        copy.start()
    for copy in copies:
        copy.wait()


def body(gradients, master_shard, first_moment, second_moment):
    grad = gradients.reshape(gradients.shape[2], gradients.shape[3])
    hbm = pl.BlockSpec(memory_space=pltpu.HBM)
    dma = pltpu.SemaphoreType.DMA
    shard = jax.ShapeDtypeStruct(master_shard.shape, F32)
    group = jax.ShapeDtypeStruct((256, 256), BF16)
    state, weights = pl.pallas_call(
        kernel,
        out_shape=(jax.ShapeDtypeStruct((3,) + master_shard.shape, F32), group),
        in_specs=[hbm] * 4,
        out_specs=(hbm,) * 2,
        scratch_shapes=[
            pltpu.VMEM((2, 8, 256, 256), BF16),
            pltpu.VMEM((2, 8, 256, 256), BF16),
            pltpu.VMEM((2, 4, 8, 4, 16, 128), BF16),
            pltpu.VMEM((2, 2, 2, 2, 4, 4, 16, 128), BF16),
            pltpu.VMEM((8, 2, 2, 4, 16, 128), BF16),
            pltpu.VMEM((7, 2, 2, 4, 16, 128), BF16),
            pltpu.VMEM((8, 2, 4, 2, 16, 128), BF16),
            pltpu.VMEM((7, 2, 4, 2, 16, 128), BF16),
            pltpu.VMEM((2, 8, 4, 16, 128), BF16),
            pltpu.VMEM((2, 7, 4, 16, 128), BF16),
            pltpu.VMEM((2, 4, 16, 128), BF16),
            pltpu.VMEM((7, 16, 128), BF16),
            pltpu.VMEM((2, 2, 2, 4, 16, 128), BF16),
            pltpu.VMEM((3, 2, 4, 16, 128), BF16),
            pltpu.VMEM((2, 8, 16, 128), BF16),
            pltpu.VMEM((2, 7, 16, 128), BF16),
            pltpu.VMEM((3, 16, 256), F32),
            pltpu.VMEM((3, 16, 256), F32),
            pltpu.VMEM((16, 256), BF16),
            dma((2, 8)), dma((3,)), dma((2,)), pltpu.SemaphoreType.REGULAR((4,)), dma((2, 2)),
            dma((1,)), dma((2, 8)),
            dma((1,)), dma((2, 2)),
            dma((1,)), dma((2,)),
            dma((1,)), dma((2,)),
            dma((1,)), dma((2,)),
            dma((1,)), dma((2,)),
            dma((1,)), dma((1,)),
            dma((1,)), dma((2,)),
            dma((1,)), dma((1,)),
        ],
        compiler_params=pltpu.CompilerParams(
            collective_id=0, has_side_effects=True, vmem_limit_bytes=52 << 20
        ),
        name="reduce_adam_gather",
    )(*[pltpu.with_memory_space_constraint(v, pltpu.HBM) for v in (grad, master_shard, first_moment, second_moment)])
    return pl.pallas_call(
        hand_out,
        out_shape=(shard, shard, shard, group),
        in_specs=[hbm] * 2,
        out_specs=(hbm,) * 4,
        scratch_shapes=[dma((4,))],
        compiler_params=pltpu.CompilerParams(vmem_limit_bytes=52 << 20),
        name="hand_out",
    )(state, weights)


def solution(mesh):
    return jax.shard_map(
        body,
        mesh=mesh,
        in_specs=(
            P("inner", "outer", None, None),
            P("outer", "inner"),
            P("outer", "inner"),
            P("outer", "inner"),
        ),
        out_specs=(P("outer", "inner"), P("outer", "inner"), P("outer", "inner"), P(None, "inner")),
        check_vma=False,
    )
```
